1024 devices in a mesh: side: 2 (over x_hi), grp: 32 (over x_lo, z), rep: 16 (over y, core).
Axes of the slice: x: 4 (x_hi: 2, x_lo: 2; x = x_hi * 2 + x_lo), y: 8, z: 16, core: 2. Of those that a mesh axis runs over, the one named last changes fastest.
Arguments:
- tokens: bfloat16 [2048, 4096], P('grp', ('side', 'rep')), may hold values from -6 to 6
- grad_out: bfloat16 [2048, 4096], P('grp', ('side', 'rep')), may hold values from -1.5 to 1.5
- route: int32 [2048, 2], P('grp'), may hold values from 0 to 31, all different within a row; in each aligned block of 64 rows (0 to 63, 64 to 127, ...) at most 8 rows name the same one
- gate: bfloat16 [2048, 2], P('grp'), may hold values from 0.099609375 to 1
- w_gate: bfloat16 [32, 4096, 4096], P('grp', None, ('side', 'rep')), may hold values from -0.09375 to 0.09375
- w_up: bfloat16 [32, 4096, 4096], P('grp', None, ('side', 'rep')), may hold values from -0.09375 to 0.09375
- w_down: bfloat16 [32, 4096, 4096], P('grp', ('side', 'rep')), may hold values from -0.09375 to 0.09375
Outputs:
- layer_out: bfloat16 [2048, 4096], P('grp', ('side', 'rep'))
- grad_tokens: bfloat16 [2048, 4096], P('grp', ('side', 'rep'))
- gate_grad: float32 [2048, 2], P('grp')
The draws below stay inside these ranges and needn't reach their ends.
Inputs may be any that keep to these rules, and one draw needn't show every extreme that they name: `route`: each row names two different experts. Within each aligned block of 64 rows no expert is named by more than 8 rows, and in some block one expert is named by exactly 8 rows.
All inputs are finite; a program needn't handle non-finite values.
Results may differ from the reference program's by a relative error of at most 0.009.
Values may be sent and summed in bfloat16 or wider, within the bound.
No kernel may reach another device: no remote copies, remote signals or barrier semaphores. Data moves between devices by JAX's collectives and lax.ppermute only.
A program may use at most 32 MiB of HBM per device.

```python
import math
import jax
import jax.numpy as jnp
import numpy as np
from jax import lax

D = 4096
FF = 4096
CAP = 8
EXPERTS = 32
TOK_G = 64
TOKENS = 2048
N_GRP = 32


def shard_levels(own_key, dims, shards, low, high):
    gain = 1.0
    for dim, parts in shards:
        steps = jax.random.uniform(jax.random.fold_in(jax.random.fold_in(own_key, 6), dim), (parts,), jnp.float32, low / len(shards), high / len(shards))
        gain = gain * jnp.repeat(jnp.exp(steps), dims[dim] // parts).reshape((-1,) + (1,) * (len(dims) - 1 - dim))
    return gain


def deal_out(rng, own, number, rows, amount, top, limit, slope):
    sequence = jax.random.permutation(rng, amount)
    crowded, common = load_shares(amount, rows * top, limit, slope, True), load_shares(amount, rows * top, limit, slope, False)
    places = jnp.arange(amount)

    def named(lengths, turn):
        used = int((lengths > 0).sum())
        fixed = max(1, used // 4)
        passed = fixed + (places - fixed + turn * (used - fixed)) % max(1, amount - fixed)
        return jnp.zeros((amount,), jnp.int32).at[sequence[jnp.where(places < fixed, places, passed)]].set(jnp.asarray(lengths, jnp.int32))

    lengths = jnp.where(number % 4 == 0, named(crowded, number // 4), named(common, number - number // 4 - 1))
    mixed = jax.random.permutation(jax.random.fold_in(own, 3), amount)
    source_of, sink = mixed[0:amount // 2 * 2:2], mixed[1:amount // 2 * 2:2]
    slack = jnp.minimum(lengths[source_of] - 1, limit - lengths[sink]) // 2
    slack = jnp.where((source_of == sequence[0]) | (sink == sequence[0]) | (lengths[sink] == 0), 0, jnp.maximum(slack, 0))
    passed = jax.random.randint(jax.random.fold_in(own, 4), (amount // 2,), 0, 1 << 20) % (slack + 1)
    lengths = lengths.at[source_of].add(-passed).at[sink].add(passed)
    labels = jnp.searchsorted(jnp.cumsum(lengths), jnp.arange(rows * top), side="right").astype(jnp.int32)
    listing = labels.reshape(top, rows).T
    listing = listing[jax.random.permutation(jax.random.fold_in(own, 1), rows)]
    turn = jax.random.randint(jax.random.fold_in(own, 2), (rows, 1), 0, top)
    return jnp.take_along_axis(listing, (jnp.arange(top)[None, :] + turn) % top, axis=1)


def load_shares(amount, total, limit, skew, full):
    loads = [(1 << 20) // math.isqrt(standing ** skew) + 1 for standing in range(1, amount + 1)]
    largest = limit if full else min(limit, max(-(-total // amount), total * loads[0] // sum(loads)))
    least = 1 if total - largest >= amount - 1 else 0
    counts, spare = [largest] + [least] * (amount - 1), total - largest - least * (amount - 1)
    while spare > 0:
        movable = [i for i in range(1, amount) if counts[i] < largest] or [i for i in range(1, amount) if counts[i] < limit]
        pool, budget = sum([loads[i] for i in movable]), spare
        for i in movable:
            addition = min(limit - counts[i], max(1, budget * loads[i] // pool), spare)
            counts[i] = counts[i] + addition
            spare = spare - addition
    return np.array(counts)


def scatter_about(key, extent, spread, limit, shards=(), kind=jnp.bfloat16):
    array = jax.random.normal(key, extent, jnp.float32) * spread
    if len(shards) > 0:
        array = shard_levels(key, extent, shards, -0.22, 0.18) * array
    return jnp.clip(array, min=-limit, max=limit).astype(kind)


def setup_inputs(seed: int = 0) -> dict:
    key_list = jax.random.split(jax.random.key(seed), 8)
    tokens = scatter_about(key_list[0], (TOKENS, D), 1.0, 6.0, ((0, 32), (1, 32)))
    grad_out = scatter_about(key_list[1], (TOKENS, D), 0.25, 1.5, ((0, 32), (1, 32)))
    route_keys = jax.random.split(jax.random.fold_in(key_list[2], 1), TOKENS // TOK_G)
    route_turns = jax.random.permutation(jax.random.fold_in(key_list[2], 3), TOKENS // TOK_G)
    route = jax.vmap(lambda own, number: deal_out(jax.random.fold_in(key_list[2], 2), own, number, TOK_G, EXPERTS, 2, CAP, 2))(route_keys, route_turns).reshape((TOKENS, 2))
    gate = jnp.clip(0.099609375 + 0.9003906 * jax.random.uniform(key_list[3], (TOKENS, 2), jnp.float32) ** shard_levels(key_list[3], (TOKENS, 2), ((0, 32),), -0.2, 0.2), 0.099609375, 1.0).astype(jnp.bfloat16)
    w_gate = scatter_about(key_list[4], (EXPERTS, D, FF), D ** -0.5, 0.09375, ((0, 32), (2, 32)))
    w_up = scatter_about(key_list[5], (EXPERTS, D, FF), D ** -0.5, 0.09375, ((0, 32), (2, 32)))
    w_down = scatter_about(key_list[6], (EXPERTS, FF, D), FF ** -0.5, 0.09375, ((0, 32), (1, 32)))
    return {"tokens": tokens, "grad_out": grad_out, "route": route, "gate": gate, "w_gate": w_gate, "w_up": w_up, "w_down": w_down}


def expert_pass(rows_x, rows_dy, coef, wg, wu, wd):
    pre_gate = jnp.dot(rows_x, wg, preferred_element_type=jnp.float32)
    pre_up = jnp.dot(rows_x, wu, preferred_element_type=jnp.float32)
    back = jnp.dot(rows_dy, wd.T, preferred_element_type=jnp.float32)
    sigma = jax.nn.sigmoid(pre_gate)
    active = pre_gate * sigma
    hidden = (active * pre_up).astype(jnp.bfloat16)
    partial_gate = jnp.sum(hidden.astype(jnp.float32) * back, axis=1)
    d_hidden = coef[:, None] * back
    d_gate = (d_hidden * pre_up * sigma * (1.0 + pre_gate * (1.0 - sigma))).astype(jnp.bfloat16)
    d_up = (d_hidden * active).astype(jnp.bfloat16)
    grad_rows = jnp.dot(d_gate, wg.T, preferred_element_type=jnp.float32) + jnp.dot(d_up, wu.T, preferred_element_type=jnp.float32)
    layer_rows = jnp.dot(hidden, wd, preferred_element_type=jnp.float32)
    return layer_rows, grad_rows, partial_gate


def reference(tokens, grad_out, route, gate, w_gate, w_up, w_down):
    flat = route.reshape(N_GRP, TOK_G * 2).astype(jnp.int32)
    onehot = (flat[:, :, None] == jnp.arange(EXPERTS, dtype=jnp.int32)[None, None, :]).astype(jnp.int32)
    earlier = jnp.cumsum(onehot, axis=1) - onehot
    slot = jnp.sum(earlier * onehot, axis=2)
    block = jnp.arange(N_GRP, dtype=jnp.int32)[:, None]
    width = N_GRP * CAP
    place = (flat * width + block * CAP + slot).reshape(-1).astype(jnp.int32)
    assign = jnp.arange(TOKENS * 2, dtype=jnp.int32)
    table = jnp.full((EXPERTS * width,), -1, jnp.int32).at[place].set(assign).reshape(EXPERTS, width)
    gate_flat = gate.reshape(-1)

    def one_expert(packed):
        index, wg, wu, wd = packed
        valid = index >= 0
        safe = jnp.where(valid, index, 0).astype(jnp.int32)
        owner = safe // 2
        rows_x = jnp.where(valid[:, None], tokens[owner], jnp.zeros((), tokens.dtype))
        rows_dy = jnp.where(valid[:, None], grad_out[owner], jnp.zeros((), grad_out.dtype))
        coef = jnp.where(valid, gate_flat[safe].astype(jnp.float32), jnp.zeros((), jnp.float32))
        return expert_pass(rows_x, rows_dy, coef, wg, wu, wd)

    layer_rows, grad_rows, partial_gate = lax.map(one_expert, (table, w_gate, w_up, w_down))
    layer_all = layer_rows.reshape(-1, D)[place].reshape(TOKENS, 2, D)
    grad_all = grad_rows.reshape(-1, D)[place].reshape(TOKENS, 2, D)
    coef_tok = gate.astype(jnp.float32)[:, :, None]
    layer_out = jnp.sum(coef_tok * layer_all, axis=1).astype(jnp.bfloat16)
    grad_tokens = jnp.sum(grad_all, axis=1).astype(jnp.bfloat16)
    gate_grad = partial_gate.reshape(-1)[place].reshape(TOKENS, 2)
    return layer_out, grad_tokens, gate_grad
```

```python
import functools

import jax
import jax.numpy as jnp
from jax import lax
from jax.experimental import pallas as pl
from jax.experimental.pallas import tpu as pltpu
from jax.sharding import PartitionSpec as P

CAP = 8
BF = jnp.bfloat16
F32 = jnp.float32
NT = (((1,), (1,)), ((), ()))
TN = (((0,), (0,)), ((), ()))
VM = pl.BlockSpec(memory_space=pltpu.VMEM)
SM = pl.BlockSpec(memory_space=pltpu.SMEM)


def slot_masks(route_ref, groups):
    rows = route_ref.shape[0]
    first, second = route_ref[:, 0:1], route_ref[:, 1:2]
    lanes = lax.broadcasted_iota(jnp.int32, (rows, 128), 1)
    hot0 = (lanes == first).astype(F32)
    hot1 = (lanes == second).astype(F32)
    below = (
        lax.broadcasted_iota(jnp.int32, (rows, rows), 1)
        < lax.broadcasted_iota(jnp.int32, (rows, rows), 0)
    ).astype(BF)
    earlier0 = jnp.dot(below, hot0.astype(BF), preferred_element_type=F32)
    earlier1 = jnp.dot(below, hot1.astype(BF), preferred_element_type=F32)
    count0 = jnp.sum(hot0, axis=0, keepdims=True)
    slot0 = jnp.sum(earlier0 * hot0, axis=1, keepdims=True).astype(jnp.int32)
    slot1 = jnp.sum((earlier1 + count0) * hot1, axis=1, keepdims=True).astype(jnp.int32)
    wide = lax.broadcasted_iota(jnp.int32, (rows, groups * CAP), 1)
    return (
        (wide == first * CAP + slot0).astype(F32),
        (wide == second * CAP + slot1).astype(F32),
    )


def dispatch_kernel(groups, tok_ref, dy_ref, route_ref, out_ref):
    mask0, mask1 = slot_masks(route_ref, groups)
    picks = (mask0 + mask1).astype(BF)
    for part, ref in enumerate((tok_ref, dy_ref)):
        rows = lax.dot_general(picks, ref[...], TN, preferred_element_type=F32)
        out_ref[:, part * CAP : (part + 1) * CAP, :] = rows.reshape(groups, CAP, -1).astype(BF)


def combine_kernel(groups, back_ref, route_ref, gate_ref, layer_ref, grad_ref, gg_ref):
    mask0, mask1 = slot_masks(route_ref, groups)
    weights = gate_ref[...].astype(F32)
    mix = (mask0 * weights[:, 0:1] + mask1 * weights[:, 1:2]).astype(BF)
    slots = groups * CAP
    back = back_ref[...].astype(F32)
    layer = back[:, 0:CAP].reshape(slots, -1).astype(BF)
    grad = back[:, CAP : 2 * CAP].reshape(slots, -1).astype(BF)
    sums = back[:, 2 * CAP :].reshape(slots, -1).astype(BF)
    layer_ref[...] = jnp.dot(mix, layer, preferred_element_type=F32).astype(BF)
    grad_ref[...] = jnp.dot(mix, grad, preferred_element_type=F32).astype(BF)
    gg0 = jnp.dot(mask0.astype(BF), sums, preferred_element_type=F32)
    gg1 = jnp.dot(mask1.astype(BF), sums, preferred_element_type=F32)
    gg_ref[...] = jnp.concatenate([gg0[:, 0:1], gg1[:, 0:1]], axis=1)


def weight_kernel(pos_ref, wg_ref, wu_ref, wd_ref, out_ref):
    other = 1 - pos_ref[1]
    sides, ys = wg_ref.shape[0], wg_ref.shape[1]
    for s in range(sides):
        for y in range(ys):
            out_ref[0, s, y] = wg_ref[s, y, other]
            out_ref[1, s, y] = wu_ref[s, y, other]
            start = pl.multiple_of(((s * ys + y) * 2 + other) * 128, 128)
            out_ref[2, s, y] = wd_ref[:, pl.ds(start, 128)]


def pre_kernel(pos_ref, x_ref, dyo_ref, dyp_ref, wg_ref, wu_ref, wd_ref, wr_ref, out_ref):
    side, core = pos_ref[0], pos_ref[1]
    ys = wg_ref.shape[1]
    f = wg_ref.shape[-1]
    gate = up = back = None
    for rel in range(2):
        sd = side if rel == 0 else 1 - side
        x = jnp.concatenate([x_ref[y, rel] for y in range(ys)], axis=1)
        dy_from = dyo_ref if rel == 0 else dyp_ref
        dy = jnp.concatenate([dy_from[y] for y in range(ys)], axis=1)
        wg = jnp.concatenate(
            [wg_ref[sd, :, core].reshape(ys * 128, f), wr_ref[0, sd].reshape(ys * 128, f)], axis=1
        )
        wu = jnp.concatenate(
            [wu_ref[sd, :, core].reshape(ys * 128, f), wr_ref[1, sd].reshape(ys * 128, f)], axis=1
        )
        own = [
            wd_ref[:, pl.ds(pl.multiple_of(((sd * ys + y) * 2 + core) * 128, 128), 128)]
            for y in range(ys)
        ]
        wd = jnp.concatenate(
            [
                jnp.concatenate(own, axis=1),
                jnp.concatenate([wr_ref[2, sd, y] for y in range(ys)], axis=1),
            ],
            axis=0,
        )
        g = jnp.dot(x, wg, preferred_element_type=F32)
        u = jnp.dot(x, wu, preferred_element_type=F32)
        b = lax.dot_general(dy, wd, NT, preferred_element_type=F32)
        gate, up, back = (g, u, b) if rel == 0 else (gate + g, up + u, back + b)
    for at, value in enumerate((gate, up, back)):
        out_ref[:, at * f : (at + 1) * f] = value[:, :f]
        out_ref[:, (3 + at) * f : (4 + at) * f] = value[:, f:]


def post_kernel(
    pos_ref, mine_ref, theirs_ref, wg_ref, wu_ref, wd_ref, wr_ref, g_ref, keep_ref, send_ref
):
    side, core = pos_ref[0], pos_ref[1]
    ys = wg_ref.shape[1]
    f = wg_ref.shape[-1]
    rows = mine_ref.shape[0]

    def total(at):
        own = mine_ref[:, at * f : (at + 1) * f] + theirs_ref[:, (3 + at) * f : (4 + at) * f]
        par = mine_ref[:, (3 + at) * f : (4 + at) * f] + theirs_ref[:, at * f : (at + 1) * f]
        return jnp.concatenate([own, par], axis=1)

    gate, up, back = total(0), total(1), total(2)
    sigma = jax.nn.sigmoid(gate)
    active = gate * sigma
    hidden = (active * up).astype(BF)
    ones = jnp.ones((8, 2 * f), F32)
    sums = lax.dot_general(
        ones,
        hidden.astype(F32) * back,
        NT,
        preferred_element_type=F32,
        precision=lax.Precision.HIGHEST,
    )
    top = lax.broadcasted_iota(jnp.int32, (8, rows // 2), 0) == 0
    packed = jnp.where(top, sums[:, : rows // 2], sums[:, rows // 2 :]).astype(BF)
    d_gate = (back * up * sigma * (1.0 + gate * (1.0 - sigma))).astype(BF)
    d_up = (back * active).astype(BF)
    both = jnp.concatenate([d_gate, d_up], axis=1)
    for rel in range(2):
        sd = side if rel == 0 else 1 - side
        for y in range(ys):
            start = pl.multiple_of(((sd * ys + y) * 2 + core) * 128, 128)
            wd = jnp.concatenate([wd_ref[:, pl.ds(start, 128)], wr_ref[2, sd, y]], axis=0)
            wgu = jnp.concatenate(
                [wg_ref[sd, y, core], wr_ref[0, sd, y], wu_ref[sd, y, core], wr_ref[1, sd, y]],
                axis=1,
            )
            layer = jnp.dot(hidden, wd, preferred_element_type=F32).astype(BF)
            if rel == 0:
                keep_ref[y] = layer
            else:
                send_ref[y] = layer
            grad = lax.dot_general(both, wgu, NT, preferred_element_type=F32)
            g_ref[y, rel * rows : (rel + 1) * rows, :] = grad.astype(BF)
    for y in range(ys):
        g_ref[y, 2 * rows :, :] = packed


def add_kernel(a_ref, b_ref, o_ref):
    o_ref[...] = (a_ref[...].astype(F32) + b_ref[...].astype(F32)).astype(BF)


def half_kernel(g_ref, keep_ref, send_ref):
    rows = keep_ref.shape[0] - 8
    acc = g_ref[0].astype(F32)
    for y in range(1, g_ref.shape[0]):
        acc = acc + g_ref[y].astype(F32)
    keep_ref[:rows] = acc[:rows]
    keep_ref[rows:] = acc[2 * rows :]
    send_ref[:rows] = acc[rows : 2 * rows].astype(BF)
    send_ref[rows:] = acc[2 * rows :].astype(BF)


def return_kernel(groups, layer_ref, keep_ref, recv_ref, out_ref):
    rows = groups * CAP
    layer = layer_ref[0].astype(F32)
    for y in range(1, layer_ref.shape[0]):
        layer = layer + layer_ref[y].astype(F32)
    both = keep_ref[...] + recv_ref[...].astype(F32)
    out_ref[:, :CAP] = layer.reshape(groups, CAP, -1).astype(BF)
    out_ref[:, CAP : 2 * CAP] = both[:rows].reshape(groups, CAP, -1).astype(BF)
    half = rows // 2
    eye = lax.broadcasted_iota(jnp.int32, (half, half), 0) == lax.broadcasted_iota(
        jnp.int32, (half, half), 1
    )
    for part in range(2):
        line = jnp.broadcast_to(both[rows + part : rows + part + 1, :], (half, half))
        column = jnp.sum(jnp.where(eye, line, 0.0), axis=1, keepdims=True)
        wide = jnp.broadcast_to(column, (half, half)).reshape(groups // 2, CAP, half)
        out_ref[part * groups // 2 : (part + 1) * groups // 2, 2 * CAP :] = wide.astype(BF)


def call(body, outs, ins, flops=0):
    shapes = [jax.ShapeDtypeStruct(s, d) for s, d in outs]
    size = sum(a.size * a.dtype.itemsize for a in ins)
    size += sum(s.size * s.dtype.itemsize for s in shapes)
    specs = [SM if a.dtype == jnp.int32 and a.ndim == 1 else VM for a in ins]
    one = len(shapes) == 1
    return pl.pallas_call(
        body,
        out_shape=shapes[0] if one else shapes,
        in_specs=specs,
        out_specs=VM if one else [VM] * len(shapes),
        compiler_params=pltpu.CompilerParams(vmem_limit_bytes=40 << 20),
        cost_estimate=pl.CostEstimate(flops=flops, bytes_accessed=size, transcendentals=0),
    )(*ins)


def local(tokens, grad_out, route, gate, w_gate, w_up, w_down):
    groups = lax.axis_size("grp")
    ys = lax.axis_size("rep") // 2
    width = tokens.shape[1]
    rows = groups * CAP
    f = w_gate.shape[2]
    rep = lax.axis_index("rep")
    pos = jnp.stack([lax.axis_index("side"), rep % 2]).astype(jnp.int32)
    columns = [[2 * y + c for y in range(ys)] for c in range(2)]
    swap_core = [(i, i ^ 1) for i in range(2 * ys)]
    swap_side = [(0, 1), (1, 0)]

    def over_y(a):
        return lax.all_to_all(a, "rep", 0, 0, tiled=True, axis_index_groups=columns)

    wg = w_gate.reshape(2, ys, 2, width, f)
    wu = w_up.reshape(2, ys, 2, width, f)
    wd = w_down.reshape(f, -1)

    send = call(
        functools.partial(dispatch_kernel, groups),
        [((groups, 2 * CAP, width), BF)],
        [tokens, grad_out, route],
    )
    w_send = call(weight_kernel, [((3, 2, ys, width, f), BF)], [pos, wg, wu, wd])
    w_recv = lax.ppermute(w_send, "rep", swap_core)
    recv = lax.all_to_all(send, "grp", 0, 0, tiled=True)
    x = recv[:, :CAP].reshape(rows, width)
    dy = recv[:, CAP:].reshape(rows, width)

    x_other = lax.ppermute(x, "side", swap_side)
    dy_own = over_y(jnp.broadcast_to(dy[None], (ys, rows, width)))
    dy_other = lax.ppermute(dy_own, "side", swap_side)
    x_pair = jnp.stack([x, x_other])
    x_all = over_y(jnp.broadcast_to(x_pair[None], (ys, 2, rows, width)))

    depth = ys * 2 * width
    mine = call(
        pre_kernel,
        [((rows, 6 * f), F32)],
        [pos, x_all, dy_own, dy_other, wg, wu, wd, w_recv],
        flops=2 * rows * depth * 2 * f * 3,
    )
    theirs = lax.ppermute(mine, "rep", swap_core)
    grads, keep, away = call(
        post_kernel,
        [((ys, 2 * rows + 8, width), BF), ((ys, rows, width), BF), ((ys, rows, width), BF)],
        [pos, mine, theirs, wg, wu, wd, w_recv],
        flops=2 * rows * depth * 2 * f * 3,
    )
    arrived = lax.ppermute(away, "side", swap_side)
    grads = over_y(grads)
    g_keep, g_send = call(
        half_kernel, [((rows + 8, width), F32), ((rows + 8, width), BF)], [grads]
    )
    g_recv = lax.ppermute(g_send, "side", swap_side)
    layer = over_y(call(add_kernel, [((ys, rows, width), BF)], [keep, arrived]))
    out = call(
        functools.partial(return_kernel, groups),
        [((groups, 3 * CAP, width), BF)],
        [layer, g_keep, g_recv],
    )
    home = lax.all_to_all(out, "grp", 0, 0, tiled=True)
    layer_out, grad_tokens, gate_grad = call(
        functools.partial(combine_kernel, groups),
        [(tokens.shape, BF), (tokens.shape, BF), (route.shape, F32)],
        [home, route, gate],
    )
    return layer_out, grad_tokens, gate_grad


def solution(mesh):
    placed = (
        P("grp", ("side", "rep")),
        P("grp", ("side", "rep")),
        P("grp", None),
        P("grp", None),
        P("grp", None, ("side", "rep")),
        P("grp", None, ("side", "rep")),
        P("grp", ("side", "rep"), None),
    )
    return jax.shard_map(
        local,
        mesh=mesh,
        in_specs=placed,
        out_specs=(P("grp", ("side", "rep")), P("grp", ("side", "rep")), P("grp", None)),
        check_vma=False,
    )
```
